32 devices in a mesh: grp: 2 (over y), seq: 4 (over z), usr: 4 (over x, core).
Axes of the slice: x: 2, y: 2, z: 4, core: 2. Of those that a mesh axis runs over, the one named last changes fastest.
Arguments:
- history_kv: bfloat16 [16, 2048, 768], P(('grp', 'usr'), 'seq'), parts along dimension 0, may hold values from -6 to 6
- candidates: bfloat16 [16, 512, 768], P(('grp', 'usr'), 'seq'), parts along dimension 0, may hold values from -6 to 6
- lengths: int32 [16], P(('grp', 'usr')), parts along dimension 0, may hold values from 256 to 2048, as said below
- w_query: bfloat16 [768, 384], replicated, may hold values from -0.21875 to 0.21875
- w_gate: bfloat16 [768, 384], replicated, may hold values from -0.21875 to 0.21875
- token_mix: bfloat16 [512, 512], P('seq'), may hold values from -0.25 to 0.25
- w_out: bfloat16 [384, 768], replicated, may hold values from -0.3125 to 0.3125
- w_up: bfloat16 [768, 2048], P(None, 'usr'), may hold values from -0.21875 to 0.21875
- w_down: bfloat16 [2048, 768], P('usr'), may hold values from -0.125 to 0.125
Outputs:
- ranked: bfloat16 [16, 512, 768], P(('grp', 'usr'), 'seq'), parts along dimension 0
The draws below stay inside these ranges and needn't reach their ends.
There are 2 independent parts, one for each index of `grp`. The reference program is written for one: setup_inputs(seed, part) draws one part's arguments, and reference() takes and returns one part's arrays. A program takes and returns all parts, laid end to end along the dimension named above; an argument that names none is the same for every part. Nothing has to cross between parts.
Inputs may be any that keep to these rules, and one draw needn't show every extreme that they name: lengths[u] counts the first valid slots of user u's history; in every draw one user has exactly 2048 and another exactly 256.
All inputs are finite; a program needn't handle non-finite values.
Results may differ from the reference program's by a relative error of at most 0.008.
Values may be sent and summed in bfloat16 or wider, within the bound.
A program may use at most 64 MiB of HBM per device.

```python
import math
import jax
import jax.numpy as jnp
from jax import lax

D = 768
HEADS = 3
DH = 128
FF = 2048
CANDS = 512
INNER = 384
USERS = 8
HIST = 2048


def draw_lengths(key, part):
    keys = jax.random.split(key, 2)
    drawn = jax.random.randint(keys[0], (USERS,), HIST // 8, HIST + 1, dtype=jnp.int32)
    order = jax.random.permutation(keys[1], jnp.arange(USERS, dtype=jnp.int32))
    positions = jnp.arange(USERS, dtype=jnp.int32)
    drawn = jnp.where(positions == order[0], HIST, drawn)
    drawn = jnp.where(positions == order[1], HIST // 8, drawn)
    return drawn.astype(jnp.int32)


def level_of(rng, extent, shards, low, top_value):
    level = 1.0
    for position, parts in shards:
        heights = jax.random.uniform(jax.random.fold_in(jax.random.fold_in(rng, 6), position), (parts,), jnp.float32, low / len(shards), top_value / len(shards))
        level = level * jnp.repeat(jnp.exp(heights), extent[position] // parts).reshape((-1,) + (1,) * (len(extent) - 1 - position))
    return level


def normal_values(key, dims, deviation, bound, shards=(), held_as=jnp.bfloat16):
    factor_of = level_of(key, dims, shards, -0.22, 0.18) if shards else 1.0
    values = jax.random.normal(key, dims, jnp.float32) * deviation * factor_of
    return jnp.minimum(jnp.maximum(values, -bound), bound).astype(held_as)


def setup_inputs(seed: int = 0, part: int = 0) -> dict:
    key_of = jax.random.split(jax.random.key(seed), 10)
    part_keys = jax.random.split(jax.random.fold_in(key_of[9], part), 10)
    history_kv = normal_values(part_keys[0], (USERS, HIST, 2 * INNER), 1.0, 6.0, ((0, 4), (1, 4)))
    candidates = normal_values(part_keys[1], (USERS, CANDS, D), 1.0, 6.0, ((0, 4), (1, 4)))
    lengths = draw_lengths(jax.random.fold_in(jax.random.fold_in(key_of[9], part), 71), part)
    w_query = normal_values(key_of[3], (D, INNER), D ** -0.5, 0.21875)
    w_gate = normal_values(key_of[4], (D, INNER), D ** -0.5, 0.21875)
    token_mix = normal_values(key_of[5], (CANDS, CANDS), CANDS ** -0.5, 0.25, ((0, 4),))
    w_out = normal_values(key_of[6], (INNER, D), INNER ** -0.5, 0.3125)
    w_up = normal_values(key_of[7], (D, FF), D ** -0.5, 0.21875, ((1, 4),))
    w_down = normal_values(key_of[8], (FF, D), FF ** -0.5, 0.125, ((0, 4),))
    return dict(history_kv=history_kv, candidates=candidates, lengths=lengths, w_query=w_query, w_gate=w_gate, token_mix=token_mix, w_out=w_out, w_up=w_up, w_down=w_down)


def rounded(values):
    return lax.optimization_barrier(values.astype(jnp.bfloat16)).astype(jnp.float32)

def layer_norm(values):
    center = values - lax.optimization_barrier(jnp.mean(values, axis=-1, keepdims=True))
    spread = lax.optimization_barrier(jnp.mean(center * center, axis=-1, keepdims=True))
    return center * lax.rsqrt(spread + 1e-05)

def reference(history_kv, candidates, lengths, w_query, w_gate, token_mix, w_out, w_up, w_down):
    inner = HEADS * DH
    scale = 1.0 / math.sqrt(DH)
    cand_f = candidates.astype(jnp.float32)
    queries = rounded(jnp.einsum('ucd,de->uce', cand_f, w_query.astype(jnp.float32)))
    block_len = math.gcd(HIST, 2048)
    block_count = HIST // block_len

    def one_user(operands):
        query_rows, cache, limit = operands
        query_heads = query_rows.reshape(CANDS, HEADS, DH)
        blocks = cache.reshape(block_count, block_len, 2 * inner)
        starts = jnp.arange(block_count, dtype=jnp.int32) * block_len

        def step(summed, item):
            block, start = item
            key_heads = block[:, :inner].astype(jnp.float32).reshape(block_len, HEADS, DH)
            value_heads = block[:, inner:].astype(jnp.float32).reshape(block_len, HEADS, DH)
            scores = jnp.einsum('chd,thd->hct', query_heads, key_heads) * scale
            positions = start + jnp.arange(block_len, dtype=jnp.int32)
            visible = positions < limit
            weights = rounded(jnp.where(visible[None, None, :], jax.nn.silu(scores), 0.0))
            contrib = jnp.einsum('hct,thd->chd', weights, value_heads).reshape(CANDS, inner)
            return (summed + contrib, None)
        summed, _ = lax.scan(step, jnp.zeros((CANDS, inner), jnp.float32), (blocks, starts))
        return summed
    attended = lax.map(one_user, (queries, history_kv, lengths))
    normed = rounded(layer_norm(attended))
    mixed = normed + jnp.einsum('cp,upe->uce', token_mix.astype(jnp.float32), normed)
    gate_values = jax.nn.silu(jnp.einsum('ucd,de->uce', cand_f, w_gate.astype(jnp.float32)))
    gated = rounded(mixed * gate_values)
    state = cand_f + jnp.einsum('uce,ed->ucd', gated, w_out.astype(jnp.float32))
    ffn_in = rounded(layer_norm(state))
    hidden = rounded(jax.nn.gelu(jnp.einsum('ucd,df->ucf', ffn_in, w_up.astype(jnp.float32))))
    ranked = state + jnp.einsum('ucf,fd->ucd', hidden, w_down.astype(jnp.float32))
    return ranked.astype(jnp.bfloat16)
```

```python
import functools
import math

import jax
import jax.numpy as jnp
from jax import lax
from jax.experimental import pallas as pl
from jax.experimental.pallas import tpu as pltpu
from jax.sharding import PartitionSpec as P

HEADS = 3
DH = 128
F32 = jnp.float32
BF16 = jnp.bfloat16
MESH = pl.DeviceIdType.MESH


def layer_norm(values):
    center = values - jnp.mean(values, axis=-1, keepdims=True)
    spread = jnp.mean(center * center, axis=-1, keepdims=True)
    return center * lax.rsqrt(spread + 1e-05)


def silu_of_double(half):
    return half + half * jnp.tanh(half)


def gelu_tanh(v):
    return 0.5 * v * (1.0 + jnp.tanh(math.sqrt(2.0 / math.pi) * (v + 0.044715 * (v * v * v))))


def dot(a, b):
    return jnp.dot(a, b, preferred_element_type=F32)


def kernel(
    seqs,
    kv_hbm, cand_hbm, len_ref, wq_hbm, wg_hbm, tm_hbm, wo_hbm, wu_hbm, wd_hbm,
    out_ref,
    kv, cand, wq, wg, tm, wo, wu, wd,
    values, queries, sums, outgoing, incoming, normed, gates, states,
    load_sem,
    q_send, q_recv, p_send, p_recv, n_send, n_recv,
    wc_send, wc_recv, wx_send, wx_recv, wy_send, wy_recv,
):
    users, rows, _ = cand.shape
    hist = kv.shape[1]
    inner = wq.shape[1]
    hidden_slots = wu.shape[0]
    g, s, u = lax.axis_index("grp"), lax.axis_index("seq"), lax.axis_index("usr")
    partner = u + 1 - 2 * lax.rem(u, 2)
    across = lax.rem(u + 2, 4)
    across_partner = lax.rem(partner + 2, 4)
    left, right = (g, s - 1, u), (g, s + 1, u)
    has_left, has_right = s > 0, s < seqs - 1

    loads = {}
    for index, (name, source, target) in enumerate((
        ("cand", cand_hbm, cand), ("wq", wq_hbm, wq), ("kv", kv_hbm, kv), ("wg", wg_hbm, wg),
        ("tm", tm_hbm, tm), ("wo", wo_hbm, wo), ("wu", wu_hbm, wu.at[u]), ("wd", wd_hbm, wd.at[u]),
    )):
        loads[name] = pltpu.make_async_copy(source, target, load_sem.at[index])
        loads[name].start()

    barrier = pltpu.get_barrier_semaphore()
    for peer in ((g, s, partner), (g, s, across), (1 - g, s, u)):
        pl.semaphore_signal(barrier, inc=1, device_id=peer, device_id_type=MESH)

    @pl.when(has_left)
    def _():
        pl.semaphore_signal(barrier, inc=1, device_id=left, device_id_type=MESH)

    @pl.when(has_right)
    def _():
        pl.semaphore_signal(barrier, inc=1, device_id=right, device_id_type=MESH)

    def remote(source, target, send, recv, device):
        return pltpu.make_async_remote_copy(
            src_ref=source, dst_ref=target, send_sem=send, recv_sem=recv,
            device_id=device, device_id_type=MESH,
        )

    weights = ((wu_hbm, wu), (wd_hbm, wd))

    def half_of(w, slot, half):
        size = weights[w][1].shape[1] // 2
        return weights[w][1].at[slot, pl.ds(pl.multiple_of(half * size, size), size)]

    def own_half(w, half):
        size = weights[w][1].shape[1] // 2
        return weights[w][0].at[pl.ds(pl.multiple_of(half * size, size), size)]

    def to_partner_own(w, slot):
        return remote(weights[w][0], weights[w][1].at[slot], wc_send.at[w, 0], wc_recv.at[w, 0], (g, s, partner))

    def to_across(w, slot):
        return remote(own_half(w, g), half_of(w, slot, g), wx_send.at[w], wx_recv.at[w], (g, s, across))

    def to_group(w, half):
        part = half_of(w, across, half)
        return remote(part, part, wy_send.at[w], wy_recv.at[w], (1 - g, s, u))

    def to_partner_far(w, slot, half, which):
        part = half_of(w, slot, half)
        return remote(part, part, wc_send.at[w, which], wc_recv.at[w, which], (g, s, partner))

    def across_arrived(w):
        to_across(w, across).wait_recv()
        to_group(w, g).start()
        to_partner_far(w, across, g, 1).start()

    def group_arrived(w):
        to_group(w, 1 - g).wait_recv()
        to_partner_far(w, across, 1 - g, 2).start()

    def gather_copy(buf, send, recv, m, block, way):
        ref = buf.at[m, block]
        return remote(ref, ref, send.at[m, block, way], recv.at[m, block], (left, right)[way])

    def gather_step(buf, send, recv, m, step):
        @pl.when(s >= step)
        def _():
            block = s - step
            gather_copy(buf, send, recv, m, block, 1).wait_recv()

            @pl.when(has_right)
            def _():
                gather_copy(buf, send, recv, m, block, 1).start()

        @pl.when(s + step < seqs)
        def _():
            block = s + step
            gather_copy(buf, send, recv, m, block, 0).wait_recv()

            @pl.when(has_left)
            def _():
                gather_copy(buf, send, recv, m, block, 0).start()

    def gather_own(buf, send, recv, m):
        @pl.when(has_right)
        def _():
            gather_copy(buf, send, recv, m, s, 1).start()

        @pl.when(has_left)
        def _():
            gather_copy(buf, send, recv, m, s, 0).start()

    def gather_finish(buf, send, recv):
        for m in range(users):
            for block in range(seqs):
                @pl.when(jnp.logical_and(block <= s, has_right))
                def _():
                    gather_copy(buf, send, recv, m, block, 1).wait_send()

                @pl.when(jnp.logical_and(block >= s, has_left))
                def _():
                    gather_copy(buf, send, recv, m, block, 0).wait_send()

    loads["cand"].wait()
    loads["wq"].wait()
    for m in range(users):
        queries[m, s] = dot(cand[m], wq[...]).astype(BF16)
        if m == 0:
            pl.semaphore_wait(
                barrier, 3 + has_left.astype(jnp.int32) + has_right.astype(jnp.int32)
            )
        gather_own(queries, q_send, q_recv, m)
    for w in range(2):
        to_across(w, u).start()
    for w in range(2):
        to_partner_own(w, u).start()

    loads["kv"].wait()
    for m in range(users):
        slots = s * hist + lax.broadcasted_iota(jnp.int32, (hist, 1), 0)
        visible = jnp.where(slots < len_ref[m], 1.0, 0.0)
        values[m] = (kv[m, :, inner:].astype(F32) * visible).astype(BF16)

    half_scale = 0.5 / math.sqrt(DH)

    def attend(m, block):
        for head in range(HEADS):
            cols = slice(head * DH, (head + 1) * DH)
            scores = lax.dot_general(
                queries[m, block, :, cols], kv[m, :, cols], (((1,), (1,)), ((), ())),
                preferred_element_type=F32,
            )
            weight = silu_of_double(scores * half_scale).astype(BF16)
            sums[m, block, :, cols] = dot(weight, values[m, :, cols])

    def partial_copy(m, block, way):
        return remote(
            outgoing.at[m, block], incoming.at[way, m, block],
            p_send.at[m, block], p_recv.at[way, m, block], (left, right)[way],
        )

    def pass_on(m, block, way, first):
        @pl.when(first)
        def _():
            outgoing[m, block] = sums[m, block].astype(BF16)

        @pl.when(jnp.logical_not(first))
        def _():
            partial_copy(m, block, way).wait_recv()
            outgoing[m, block] = (sums[m, block] + incoming[way, m, block].astype(F32)).astype(BF16)

        partial_copy(m, block, way).start()

    mirror = seqs - 1 - s
    for step in range(max(2 * seqs - 2, seqs)):
        for m in range(users):
            if 0 < step < seqs:
                gather_step(queries, q_send, q_recv, m, step)
            if step < seqs:
                @pl.when(s >= step)
                def _():
                    attend(m, s - step)

                if step > 0:
                    @pl.when(s + step < seqs)
                    def _():
                        attend(m, s + step)

            block = step - s

            @pl.when(jnp.logical_and(block > s, block < seqs))
            def _():
                pass_on(m, block, 1, s == 0)

            far = step - mirror

            @pl.when(jnp.logical_and(far > mirror, far < seqs))
            def _():
                pass_on(m, seqs - 1 - far, 0, mirror == 0)

        if step == 0:
            loads["wg"].wait()
            for m in range(users):
                gates[m] = silu_of_double(dot(cand[m], wg[...]) * 0.5)
        if step == seqs - 1:
            across_arrived(0)

    for m in range(users):
        @pl.when(has_left)
        def _():
            partial_copy(m, s, 1).wait_recv()
            sums[m, s] = sums[m, s] + incoming[1, m, s].astype(F32)

        @pl.when(has_right)
        def _():
            partial_copy(m, s, 0).wait_recv()
            sums[m, s] = sums[m, s] + incoming[0, m, s].astype(F32)

        normed[m, s] = layer_norm(sums[m, s]).astype(BF16)
        gather_own(normed, n_send, n_recv, m)
    across_arrived(1)
    for step in range(1, seqs):
        for m in range(users):
            gather_step(normed, n_send, n_recv, m, step)
        if step == 1:
            group_arrived(0)

    loads["tm"].wait()
    loads["wo"].wait()
    ffn_ins = []
    for m in range(users):
        mixed = normed[m, s].astype(F32)
        for block in range(seqs):
            mixed = mixed + dot(tm[:, block * rows:(block + 1) * rows], normed[m, block])
        gated = (mixed * gates[m]).astype(BF16)
        state = cand[m].astype(F32) + dot(gated, wo[...])
        states[m * rows:(m + 1) * rows] = state
        ffn_ins.append(layer_norm(state).astype(BF16))
    ffn_in = jnp.concatenate(ffn_ins, axis=0)

    group_arrived(1)
    for w in range(2):
        loads[("wu", "wd")[w]].wait()
        to_partner_own(w, partner).wait_recv()
        to_partner_far(w, across_partner, g, 1).wait_recv()
        to_partner_far(w, across_partner, 1 - g, 2).wait_recv()
    total = states[...]
    for slot in range(hidden_slots):
        hidden = gelu_tanh(dot(ffn_in, wu[slot])).astype(BF16)
        total = total + dot(hidden, wd[slot])
    for m in range(users):
        out_ref[m] = total[m * rows:(m + 1) * rows].astype(BF16)

    gather_finish(queries, q_send, q_recv)
    gather_finish(normed, n_send, n_recv)
    for m in range(users):
        for block in range(seqs):
            @pl.when(block != s)
            def _():
                partial_copy(m, block, 1).wait_send()
    for w in range(2):
        to_across(w, u).wait_send()
        to_partner_own(w, u).wait_send()
        to_group(w, g).wait_send()
        to_partner_far(w, across, g, 1).wait_send()
        to_partner_far(w, across, 1 - g, 2).wait_send()


def fused(seqs, usrs, history_kv, candidates, lengths, w_query, w_gate, token_mix, w_out, w_up, w_down):
    users, hist, _ = history_kv.shape
    rows, width = candidates.shape[1:]
    inner = w_query.shape[1]
    depth = w_up.shape[1]
    dma = pltpu.SemaphoreType.DMA
    hbm = pl.BlockSpec(memory_space=pl.ANY)
    smem = pl.BlockSpec(memory_space=pltpu.SMEM)
    return pl.pallas_call(
        functools.partial(kernel, seqs),
        out_shape=jax.ShapeDtypeStruct(candidates.shape, BF16),
        in_specs=[hbm, hbm, smem, hbm, hbm, hbm, hbm, hbm, hbm],
        out_specs=pl.BlockSpec(memory_space=pltpu.VMEM),
        scratch_shapes=[
            pltpu.VMEM(history_kv.shape, BF16),
            pltpu.VMEM(candidates.shape, BF16),
            pltpu.VMEM(w_query.shape, BF16),
            pltpu.VMEM(w_gate.shape, BF16),
            pltpu.VMEM(token_mix.shape, BF16),
            pltpu.VMEM(w_out.shape, BF16),
            pltpu.VMEM((usrs, width, depth), BF16),
            pltpu.VMEM((usrs, depth, width), BF16),
            pltpu.VMEM((users, hist, inner), BF16),
            pltpu.VMEM((users, seqs, rows, inner), BF16),
            pltpu.VMEM((users, seqs, rows, inner), F32),
            pltpu.VMEM((users, seqs, rows, inner), BF16),
            pltpu.VMEM((2, users, seqs, rows, inner), BF16),
            pltpu.VMEM((users, seqs, rows, inner), BF16),
            pltpu.VMEM((users, rows, inner), F32),
            pltpu.VMEM((users * rows, width), F32),
            dma((8,)),
            dma((users, seqs, 2)), dma((users, seqs)),
            dma((users, seqs)), dma((2, users, seqs)),
            dma((users, seqs, 2)), dma((users, seqs)),
            dma((2, 3)), dma((2, 3)), dma((2,)), dma((2,)), dma((2,)), dma((2,)),
        ],
        compiler_params=pltpu.CompilerParams(
            collective_id=0, has_side_effects=True, vmem_limit_bytes=56 * 1024 * 1024
        ),
        name="rank_layer",
    )(history_kv, candidates, lengths, w_query, w_gate, token_mix, w_out, w_up, w_down)


def shards(history_kv, candidates, lengths, w_query, w_gate, token_mix, w_out, w_up, w_down):
    user_count, hist_dev, _ = history_kv.shape
    inner = w_query.shape[1]
    half = hist_dev // 2
    scale = 1.0 / math.sqrt(DH)
    seq_index = lax.axis_index("seq")
    first_start = seq_index * hist_dev
    sections = ((history_kv[:, :half], first_start), (history_kv[:, half:], first_start + half))
    offsets = lax.iota(jnp.int32, half)
    queries = jnp.einsum(
        "ucd,de->uce", candidates, w_query, preferred_element_type=jnp.float32
    ).astype(jnp.bfloat16)
    piece = lax.all_gather(queries, "seq", axis=1, tiled=True)
    row_count = piece.shape[1]
    results = []
    for member in range(user_count):
        query_heads = piece[member].reshape(row_count, HEADS, DH)
        limit = lengths[member]
        summed = jnp.zeros((row_count, inner), jnp.float32)
        for section, section_start in sections:
            key_heads = section[member, :, :inner].reshape(half, HEADS, DH)
            value_heads = section[member, :, inner:].reshape(half, HEADS, DH)

            def compute(
                operand,
                key_heads=key_heads,
                value_heads=value_heads,
                section_start=section_start,
                query_heads=query_heads,
                limit=limit,
            ):
                scores = (
                    jnp.einsum(
                        "chd,thd->hct", query_heads, key_heads, preferred_element_type=jnp.float32
                    )
                    * scale
                )
                visible = section_start + offsets < limit
                weights = jnp.where(visible[None, None, :], jax.nn.silu(scores), 0.0).astype(
                    jnp.bfloat16
                )
                contrib = jnp.einsum(
                    "hct,thd->chd", weights, value_heads, preferred_element_type=jnp.float32
                )
                return contrib.reshape(row_count, inner)

            def skipped(operand):
                return jnp.zeros((row_count, inner), jnp.float32)

            summed = summed + lax.cond(section_start < limit, compute, skipped, 0)
        results.append(summed)
    partial_sums = jnp.stack(results)
    attended = lax.psum_scatter(partial_sums, "seq", scatter_dimension=1, tiled=True)
    normed = layer_norm(attended).astype(jnp.bfloat16)
    mixed = normed.astype(jnp.float32) + jnp.einsum(
        "cp,upe->uce",
        token_mix,
        lax.all_gather(normed, "seq", axis=1, tiled=True),
        preferred_element_type=jnp.float32,
    )
    gate_values = jax.nn.silu(
        jnp.einsum("ucd,de->uce", candidates, w_gate, preferred_element_type=jnp.float32)
    )
    gated = (mixed * gate_values).astype(jnp.bfloat16)
    state = candidates.astype(jnp.float32) + jnp.einsum(
        "uce,ed->ucd", gated, w_out, preferred_element_type=jnp.float32
    )
    ffn_in = layer_norm(state).astype(jnp.bfloat16)
    hidden = jax.nn.gelu(
        jnp.einsum(
            "ucd,df->ucf",
            lax.all_gather(ffn_in, "usr", axis=0, tiled=True),
            w_up,
            preferred_element_type=jnp.float32,
        )
    ).astype(jnp.bfloat16)
    ffn_terms = jnp.einsum("ucf,fd->ucd", hidden, w_down, preferred_element_type=jnp.float32)
    ffn_out = lax.psum_scatter(
        ffn_terms.astype(jnp.bfloat16), "usr", scatter_dimension=0, tiled=True
    ).astype(jnp.float32)
    return (state + ffn_out).astype(jnp.bfloat16)


def solution(mesh):
    sizes = dict(mesh.shape)
    seqs, usrs = sizes["seq"], sizes["usr"]
    if sizes["grp"] == 2 and usrs == 4 and 2 <= seqs <= 8:
        body = functools.partial(fused, seqs, usrs)
    else:
        body = shards
    return jax.shard_map(
        body,
        mesh=mesh,
        in_specs=(
            P(("grp", "usr"), "seq", None),
            P(("grp", "usr"), "seq", None),
            P(("grp", "usr")),
            P(),
            P(),
            P("seq", None),
            P(),
            P(None, "usr"),
            P("usr", None),
        ),
        out_specs=P(("grp", "usr"), "seq", None),
        check_vma=False,
    )
```

```python
import functools
import math

import jax
import jax.numpy as jnp
from jax import lax
from jax.experimental import pallas as pl
from jax.experimental.pallas import tpu as pltpu
from jax.sharding import PartitionSpec as P

HEADS = 3
DH = 128
F32 = jnp.float32
BF16 = jnp.bfloat16
MESH = pl.DeviceIdType.MESH
ACROSS_STEPS = (1, 2, 3, 4)
GROUP_STEPS = (3, 4, 5, 6)
MIX_STEP = 2


def layer_norm(values):
    center = values - jnp.mean(values, axis=-1, keepdims=True)
    spread = jnp.mean(center * center, axis=-1, keepdims=True)
    return center * lax.rsqrt(spread + 1e-05)


def silu_of_double(half):
    return half + half * jnp.tanh(half)


def gelu_tanh(v):
    return 0.5 * v * (1.0 + jnp.tanh(math.sqrt(2.0 / math.pi) * (v + 0.044715 * (v * v * v))))


def dot(a, b):
    return jnp.dot(a, b, preferred_element_type=F32)


def kernel(
    seqs,
    kv_hbm, cand_hbm, len_ref, wq_hbm, wg_hbm, tm_hbm, wo_hbm, wu_hbm, wd_hbm,
    out_ref,
    kv, cand, wq, wg, tm, wo, wu, wd,
    values, queries, sums, outgoing, incoming, normed, mixed_out, mixed_in, gates, states,
    load_sem,
    q_send, q_recv, p_send, p_recv, t_send, t_recv, m_send, m_recv,
    wo_send, wo_recv, wc_send, wc_recv, wx_send, wx_recv, wy_send, wy_recv,
):
    users, rows, _ = cand.shape
    hist = kv.shape[1]
    inner = wq.shape[1]
    hidden_slots = wu.shape[0]
    g, s, u = lax.axis_index("grp"), lax.axis_index("seq"), lax.axis_index("usr")
    partner = u + 1 - 2 * lax.rem(u, 2)
    across = lax.rem(u + 2, 4)
    across_partner = lax.rem(partner + 2, 4)
    left, right = (g, s - 1, u), (g, s + 1, u)
    has_left, has_right = s > 0, s < seqs - 1

    first_owned = lax.rem(u, 2) * users
    owned = s - first_owned
    is_owner = jnp.logical_and(owned >= 0, owned < users)

    loads = {}
    for index, (name, source, target) in enumerate((
        ("cand", cand_hbm, cand), ("wq", wq_hbm, wq), ("kv", kv_hbm, kv), ("wg", wg_hbm, wg),
        ("tm", tm_hbm, tm.at[s]), ("wo", wo_hbm, wo), ("wu", wu_hbm, wu.at[u]), ("wd", wd_hbm, wd.at[u]),
    )):
        loads[name] = pltpu.make_async_copy(source, target, load_sem.at[index])
        loads[name].start()

    barrier = pltpu.get_barrier_semaphore()
    peers = [(g, s, partner), (g, s, across), (1 - g, s, u)]
    peers += [(g, lax.rem(s + step, seqs), u) for step in range(1, seqs)]
    for peer in peers:
        pl.semaphore_signal(barrier, inc=1, device_id=peer, device_id_type=MESH)

    def remote(source, target, send, recv, device):
        return pltpu.make_async_remote_copy(
            src_ref=source, dst_ref=target, send_sem=send, recv_sem=recv,
            device_id=device, device_id_type=MESH,
        )

    weights = ((wu_hbm, wu), (wd_hbm, wd))

    def rows_of(piece, half):
        size = weights[piece // 2][1].shape[1] // 4
        return pl.ds(pl.multiple_of((half * 2 + piece % 2) * size, size), size)

    def piece_of(piece, slot, half):
        return weights[piece // 2][1].at[slot, rows_of(piece, half)]

    def to_partner_own(w, slot):
        return remote(weights[w][0], weights[w][1].at[slot], wo_send.at[w], wo_recv.at[w], (g, s, partner))

    def to_across(piece, slot):
        source = weights[piece // 2][0].at[rows_of(piece, g)]
        return remote(source, piece_of(piece, slot, g), wx_send.at[piece], wx_recv.at[piece], (g, s, across))

    def to_group(piece, half):
        part = piece_of(piece, across, half)
        return remote(part, part, wy_send.at[piece], wy_recv.at[piece], (1 - g, s, u))

    def to_partner_far(piece, slot, half, which):
        part = piece_of(piece, slot, half)
        return remote(part, part, wc_send.at[piece, which], wc_recv.at[piece, which], (g, s, partner))

    def across_arrived(piece):
        to_across(piece, across).wait_recv()
        to_group(piece, g).start()
        to_partner_far(piece, across, g, 0).start()

    def group_arrived(piece):
        to_group(piece, 1 - g).wait_recv()
        to_partner_far(piece, across, 1 - g, 1).start()

    def gather_copy(buf, send, recv, m, block, way):
        ref = buf.at[m, block]
        return remote(ref, ref, send.at[m, block, way], recv.at[m, block], (left, right)[way])

    def gather_step(buf, send, recv, m, step):
        @pl.when(s >= step)
        def _():
            block = s - step
            gather_copy(buf, send, recv, m, block, 1).wait_recv()

            @pl.when(has_right)
            def _():
                gather_copy(buf, send, recv, m, block, 1).start()

        @pl.when(s + step < seqs)
        def _():
            block = s + step
            gather_copy(buf, send, recv, m, block, 0).wait_recv()

            @pl.when(has_left)
            def _():
                gather_copy(buf, send, recv, m, block, 0).start()

    def gather_own(buf, send, recv, m):
        @pl.when(has_right)
        def _():
            gather_copy(buf, send, recv, m, s, 1).start()

        @pl.when(has_left)
        def _():
            gather_copy(buf, send, recv, m, s, 0).start()

    def gather_finish(buf, send, recv):
        for m in range(users):
            for block in range(seqs):
                @pl.when(jnp.logical_and(block <= s, has_right))
                def _():
                    gather_copy(buf, send, recv, m, block, 1).wait_send()

                @pl.when(jnp.logical_and(block >= s, has_left))
                def _():
                    gather_copy(buf, send, recv, m, block, 0).wait_send()

    loads["cand"].wait()
    loads["wq"].wait()
    for m in range(users):
        queries[m, s] = dot(cand[m], wq[...]).astype(BF16)
        if m == 0:
            pl.semaphore_wait(barrier, len(peers))
        gather_own(queries, q_send, q_recv, m)
    for piece in range(4):
        to_across(piece, u).start()
    for w in range(2):
        to_partner_own(w, u).start()

    loads["kv"].wait()
    for m in range(users):
        slots = s * hist + lax.broadcasted_iota(jnp.int32, (hist, 1), 0)
        visible = jnp.where(slots < len_ref[m], 1.0, 0.0)
        values[m] = (kv[m, :, inner:].astype(F32) * visible).astype(BF16)

    half_scale = 0.5 / math.sqrt(DH)

    def attend(m, block):
        for head in range(HEADS):
            cols = slice(head * DH, (head + 1) * DH)
            scores = lax.dot_general(
                queries[m, block, :, cols], kv[m, :, cols], (((1,), (1,)), ((), ())),
                preferred_element_type=F32,
            )
            weight = silu_of_double(scores * half_scale).astype(BF16)
            sums[m, block, :, cols] = dot(weight, values[m, :, cols])

    def partial_copy(m, block, way):
        return remote(
            outgoing.at[m, block], incoming.at[way, m, block],
            p_send.at[m, block], p_recv.at[way, m, block], (left, right)[way],
        )

    def pass_on(m, block, way, first):
        @pl.when(first)
        def _():
            outgoing[m, block] = sums[m, block].astype(BF16)

        @pl.when(jnp.logical_not(first))
        def _():
            partial_copy(m, block, way).wait_recv()
            outgoing[m, block] = (sums[m, block] + incoming[way, m, block].astype(F32)).astype(BF16)

        partial_copy(m, block, way).start()

    def mix_copy(m):
        return remote(tm_hbm, tm.at[s], t_send.at[m], t_recv.at[s], (g, first_owned + m, u))

    mirror = seqs - 1 - s
    for step in range(2 * seqs - 2):
        for m in range(users):
            if 0 < step < seqs:
                gather_step(queries, q_send, q_recv, m, step)
            if step < seqs:
                @pl.when(s >= step)
                def _():
                    attend(m, s - step)

                if step > 0:
                    @pl.when(s + step < seqs)
                    def _():
                        attend(m, s + step)

            owner = first_owned + m
            block = step - s

            @pl.when((owner > s) & (block >= 0) & (block < seqs))
            def _():
                pass_on(m, block, 1, s == 0)

            far = step - mirror

            @pl.when((owner < s) & (far >= 0) & (far < seqs))
            def _():
                pass_on(m, seqs - 1 - far, 0, mirror == 0)

        if step == 0:
            loads["wg"].wait()
            for m in range(users):
                gates[m] = silu_of_double(dot(cand[m], wg[...]) * 0.5)
        if step == MIX_STEP:
            for m in range(users):
                @pl.when(first_owned + m != s)
                def _():
                    mix_copy(m).start()
        for piece in range(4):
            if step == ACROSS_STEPS[piece]:
                across_arrived(piece)
            if step == GROUP_STEPS[piece]:
                group_arrived(piece)

    def mixed_copy(block, m):
        return remote(
            mixed_out.at[block], mixed_in.at[m], m_send.at[block], m_recv.at[m], (g, block, u)
        )

    order = sorted(range(seqs), key=lambda block: min(block, seqs - 1 - block))
    loads["tm"].wait()

    @pl.when(is_owner)
    def _():
        for block in range(seqs):
            @pl.when(has_left)
            def _():
                partial_copy(owned, block, 1).wait_recv()
                sums[owned, block] = sums[owned, block] + incoming[1, owned, block].astype(F32)

            @pl.when(has_right)
            def _():
                partial_copy(owned, block, 0).wait_recv()
                sums[owned, block] = sums[owned, block] + incoming[0, owned, block].astype(F32)

            normed[block * rows:(block + 1) * rows] = layer_norm(sums[owned, block]).astype(BF16)
        for block in range(seqs):
            @pl.when(block != s)
            def _():
                remote(
                    tm_hbm, tm.at[block], t_send.at[0], t_recv.at[block], (g, lax.rem(s + 1, seqs), u)
                ).wait_recv()
        for block in order:
            mixed = normed[block * rows:(block + 1) * rows].astype(F32) + dot(tm[block], normed[...])
            mixed_out[block] = mixed.astype(BF16)

            @pl.when(block != s)
            def _():
                mixed_copy(block, owned).start()

            @pl.when(block == s)
            def _():
                mixed_in[owned] = mixed.astype(BF16)

    for piece in range(4):
        if GROUP_STEPS[piece] >= 2 * seqs - 2:
            group_arrived(piece)
    loads["wo"].wait()
    ffn_ins = []
    for m in range(users):
        @pl.when(first_owned + m != s)
        def _():
            mixed_copy(s, m).wait_recv()

        gated = (mixed_in[m].astype(F32) * gates[m]).astype(BF16)
        state = cand[m].astype(F32) + dot(gated, wo[...])
        states[m * rows:(m + 1) * rows] = state
        ffn_ins.append(layer_norm(state).astype(BF16))
    ffn_in = jnp.concatenate(ffn_ins, axis=0)

    for w in range(2):
        loads[("wu", "wd")[w]].wait()
        to_partner_own(w, partner).wait_recv()
    for piece in range(4):
        to_partner_far(piece, across_partner, g, 0).wait_recv()
        to_partner_far(piece, across_partner, 1 - g, 1).wait_recv()
    total = states[...]
    for slot in range(hidden_slots):
        hidden = gelu_tanh(dot(ffn_in, wu[slot])).astype(BF16)
        total = total + dot(hidden, wd[slot])
    for m in range(users):
        out_ref[m] = total[m * rows:(m + 1) * rows].astype(BF16)

    gather_finish(queries, q_send, q_recv)
    for m in range(users):
        @pl.when(first_owned + m != s)
        def _():
            mix_copy(m).wait_send()
            for block in range(seqs):
                partial_copy(m, block, 1).wait_send()

    @pl.when(is_owner)
    def _():
        for block in range(seqs):
            @pl.when(block != s)
            def _():
                mixed_copy(block, owned).wait_send()

    for w in range(2):
        to_partner_own(w, u).wait_send()
    for piece in range(4):
        to_across(piece, u).wait_send()
        to_group(piece, g).wait_send()
        to_partner_far(piece, across, g, 0).wait_send()
        to_partner_far(piece, across, 1 - g, 1).wait_send()


def fused(seqs, usrs, history_kv, candidates, lengths, w_query, w_gate, token_mix, w_out, w_up, w_down):
    users, hist, _ = history_kv.shape
    rows, width = candidates.shape[1:]
    inner = w_query.shape[1]
    depth = w_up.shape[1]
    dma = pltpu.SemaphoreType.DMA
    hbm = pl.BlockSpec(memory_space=pl.ANY)
    smem = pl.BlockSpec(memory_space=pltpu.SMEM)
    return pl.pallas_call(
        functools.partial(kernel, seqs),
        out_shape=jax.ShapeDtypeStruct(candidates.shape, BF16),
        in_specs=[hbm, hbm, smem, hbm, hbm, hbm, hbm, hbm, hbm],
        out_specs=pl.BlockSpec(memory_space=pltpu.VMEM),
        scratch_shapes=[
            pltpu.VMEM(history_kv.shape, BF16),
            pltpu.VMEM(candidates.shape, BF16),
            pltpu.VMEM(w_query.shape, BF16),
            pltpu.VMEM(w_gate.shape, BF16),
            pltpu.VMEM((seqs, *token_mix.shape), BF16),
            pltpu.VMEM(w_out.shape, BF16),
            pltpu.VMEM((usrs, width, depth), BF16),
            pltpu.VMEM((usrs, depth, width), BF16),
            pltpu.VMEM((users, hist, inner), BF16),
            pltpu.VMEM((users, seqs, rows, inner), BF16),
            pltpu.VMEM((users, seqs, rows, inner), F32),
            pltpu.VMEM((users, seqs, rows, inner), BF16),
            pltpu.VMEM((2, users, seqs, rows, inner), BF16),
            pltpu.VMEM((seqs * rows, inner), BF16),
            pltpu.VMEM((seqs, rows, inner), BF16),
            pltpu.VMEM((users, rows, inner), BF16),
            pltpu.VMEM((users, rows, inner), F32),
            pltpu.VMEM((users * rows, width), F32),
            dma((8,)),
            dma((users, seqs, 2)), dma((users, seqs)),
            dma((users, seqs)), dma((2, users, seqs)),
            dma((users,)), dma((seqs,)), dma((seqs,)), dma((users,)),
            dma((2,)), dma((2,)), dma((4, 2)), dma((4, 2)),
            dma((4,)), dma((4,)), dma((4,)), dma((4,)),
        ],
        compiler_params=pltpu.CompilerParams(
            collective_id=0, has_side_effects=True, vmem_limit_bytes=56 * 1024 * 1024
        ),
        name="rank_layer",
    )(history_kv, candidates, lengths, w_query, w_gate, token_mix, w_out, w_up, w_down)


def shards(history_kv, candidates, lengths, w_query, w_gate, token_mix, w_out, w_up, w_down):
    user_count, hist_dev, _ = history_kv.shape
    inner = w_query.shape[1]
    half = hist_dev // 2
    scale = 1.0 / math.sqrt(DH)
    seq_index = lax.axis_index("seq")
    first_start = seq_index * hist_dev
    sections = ((history_kv[:, :half], first_start), (history_kv[:, half:], first_start + half))
    offsets = lax.iota(jnp.int32, half)
    queries = jnp.einsum(
        "ucd,de->uce", candidates, w_query, preferred_element_type=jnp.float32
    ).astype(jnp.bfloat16)
    piece = lax.all_gather(queries, "seq", axis=1, tiled=True)
    row_count = piece.shape[1]
    results = []
    for member in range(user_count):
        query_heads = piece[member].reshape(row_count, HEADS, DH)
        limit = lengths[member]
        summed = jnp.zeros((row_count, inner), jnp.float32)
        for section, section_start in sections:
            key_heads = section[member, :, :inner].reshape(half, HEADS, DH)
            value_heads = section[member, :, inner:].reshape(half, HEADS, DH)

            def compute(
                operand,
                key_heads=key_heads,
                value_heads=value_heads,
                section_start=section_start,
                query_heads=query_heads,
                limit=limit,
            ):
                scores = (
                    jnp.einsum(
                        "chd,thd->hct", query_heads, key_heads, preferred_element_type=jnp.float32
                    )
                    * scale
                )
                visible = section_start + offsets < limit
                weights = jnp.where(visible[None, None, :], jax.nn.silu(scores), 0.0).astype(
                    jnp.bfloat16
                )
                contrib = jnp.einsum(
                    "hct,thd->chd", weights, value_heads, preferred_element_type=jnp.float32
                )
                return contrib.reshape(row_count, inner)

            def skipped(operand):
                return jnp.zeros((row_count, inner), jnp.float32)

            summed = summed + lax.cond(section_start < limit, compute, skipped, 0)
        results.append(summed)
    partial_sums = jnp.stack(results)
    attended = lax.psum_scatter(partial_sums, "seq", scatter_dimension=1, tiled=True)
    normed = layer_norm(attended).astype(jnp.bfloat16)
    mixed = normed.astype(jnp.float32) + jnp.einsum(
        "cp,upe->uce",
        token_mix,
        lax.all_gather(normed, "seq", axis=1, tiled=True),
        preferred_element_type=jnp.float32,
    )
    gate_values = jax.nn.silu(
        jnp.einsum("ucd,de->uce", candidates, w_gate, preferred_element_type=jnp.float32)
    )
    gated = (mixed * gate_values).astype(jnp.bfloat16)
    state = candidates.astype(jnp.float32) + jnp.einsum(
        "uce,ed->ucd", gated, w_out, preferred_element_type=jnp.float32
    )
    ffn_in = layer_norm(state).astype(jnp.bfloat16)
    hidden = jax.nn.gelu(
        jnp.einsum(
            "ucd,df->ucf",
            lax.all_gather(ffn_in, "usr", axis=0, tiled=True),
            w_up,
            preferred_element_type=jnp.float32,
        )
    ).astype(jnp.bfloat16)
    ffn_terms = jnp.einsum("ucf,fd->ucd", hidden, w_down, preferred_element_type=jnp.float32)
    ffn_out = lax.psum_scatter(
        ffn_terms.astype(jnp.bfloat16), "usr", scatter_dimension=0, tiled=True
    ).astype(jnp.float32)
    return (state + ffn_out).astype(jnp.bfloat16)


def solution(mesh):
    sizes = dict(mesh.shape)
    seqs, usrs = sizes["seq"], sizes["usr"]
    def body(history_kv, candidates, *rest):
        operands = (history_kv, candidates, *rest)
        if sizes["grp"] == 2 and usrs == 4 and seqs == 2 * candidates.shape[0] and seqs >= 4:
            return fused(seqs, usrs, *operands)
        return shards(*operands)

    return jax.shard_map(
        body,
        mesh=mesh,
        in_specs=(
            P(("grp", "usr"), "seq", None),
            P(("grp", "usr"), "seq", None),
            P(("grp", "usr")),
            P(),
            P(),
            P("seq", None),
            P(),
            P(None, "usr"),
            P("usr", None),
        ),
        out_specs=P(("grp", "usr"), "seq", None),
        check_vma=False,
    )
```

```python
import functools
import math

import jax
import jax.numpy as jnp
from jax import lax
from jax.experimental import pallas as pl
from jax.experimental.pallas import tpu as pltpu
from jax.sharding import PartitionSpec as P

HEADS = 3
DH = 128
F32 = jnp.float32
BF16 = jnp.bfloat16
MESH = pl.DeviceIdType.MESH
ACROSS_STEPS = (1, 2, 3, 4)
GROUP_STEPS = (3, 4, 5, 6)
MIX_STEP = 0
SHARE_STEPS = (3, 4)


def layer_norm(values):
    center = values - jnp.mean(values, axis=-1, keepdims=True)
    spread = jnp.mean(center * center, axis=-1, keepdims=True)
    return center * lax.rsqrt(spread + 1e-05)


def silu_of_double(half):
    return half + half * jnp.tanh(half)


def gelu_tanh(v):
    return 0.5 * v * (1.0 + jnp.tanh(math.sqrt(2.0 / math.pi) * (v + 0.044715 * (v * v * v))))


def dot(a, b):
    return jnp.dot(a, b, preferred_element_type=F32)


def kernel(
    seqs,
    kv_hbm, cand_hbm, len_ref, wq_hbm, wg_hbm, tm_hbm, wo_hbm, wu_hbm, wd_hbm,
    out_ref,
    kv, cand, wq, wg, tm, wo, wu, wd,
    values, queries, sums, outgoing, incoming, normed, mixed_out, mixed_in, gates, states,
    load_sem,
    q_send, q_recv, p_send, p_recv, t_send, t_recv, f_send, m_send, m_recv,
    wo_send, wo_recv, wc_send, wc_recv, wx_send, wx_recv, wy_send, wy_recv,
):
    users, rows, _ = cand.shape
    hist = kv.shape[1]
    inner = wq.shape[1]
    hidden_slots = wu.shape[0]
    g, s, u = lax.axis_index("grp"), lax.axis_index("seq"), lax.axis_index("usr")
    partner = u + 1 - 2 * lax.rem(u, 2)
    across = lax.rem(u + 2, 4)
    across_partner = lax.rem(partner + 2, 4)
    left, right = (g, s - 1, u), (g, s + 1, u)
    has_left, has_right = s > 0, s < seqs - 1

    first_owned = lax.rem(u, 2) * users
    owned = s - first_owned
    is_owner = jnp.logical_and(owned >= 0, owned < users)

    loads = {}
    for index, (name, source, target) in enumerate((
        ("cand", cand_hbm, cand), ("wq", wq_hbm, wq), ("kv", kv_hbm, kv), ("wg", wg_hbm, wg),
        ("tm", tm_hbm, tm.at[s]), ("wo", wo_hbm, wo), ("wu", wu_hbm, wu.at[u]), ("wd", wd_hbm, wd.at[u]),
    )):
        loads[name] = pltpu.make_async_copy(source, target, load_sem.at[index])

    for name in ("cand", "wq"):
        loads[name].start()

    barrier = pltpu.get_barrier_semaphore()
    peers = [(g, s, partner), (g, s, across), (1 - g, s, u)]
    peers += [(g, lax.rem(s + step, seqs), u) for step in range(1, seqs)]
    for peer in peers:
        pl.semaphore_signal(barrier, inc=1, device_id=peer, device_id_type=MESH)

    def remote(source, target, send, recv, device):
        return pltpu.make_async_remote_copy(
            src_ref=source, dst_ref=target, send_sem=send, recv_sem=recv,
            device_id=device, device_id_type=MESH,
        )

    weights = ((wu_hbm, wu), (wd_hbm, wd))

    def rows_of(piece, half):
        size = weights[piece // 2][1].shape[1] // 4
        return pl.ds(pl.multiple_of((half * 2 + piece % 2) * size, size), size)

    def piece_of(piece, slot, half):
        return weights[piece // 2][1].at[slot, rows_of(piece, half)]

    def to_partner_own(w, slot):
        return remote(weights[w][0], weights[w][1].at[slot], wo_send.at[w], wo_recv.at[w], (g, s, partner))

    def to_across(piece, slot):
        source = weights[piece // 2][0].at[rows_of(piece, g)]
        return remote(source, piece_of(piece, slot, g), wx_send.at[piece], wx_recv.at[piece], (g, s, across))

    def to_group(piece, half):
        part = piece_of(piece, across, half)
        return remote(part, part, wy_send.at[piece], wy_recv.at[piece], (1 - g, s, u))

    def to_partner_far(piece, slot, half, which):
        part = piece_of(piece, slot, half)
        return remote(part, part, wc_send.at[piece, which], wc_recv.at[piece, which], (g, s, partner))

    def across_arrived(piece):
        to_across(piece, across).wait_recv()
        to_group(piece, g).start()
        to_partner_far(piece, across, g, 0).start()

    def group_arrived(piece):
        to_group(piece, 1 - g).wait_recv()
        to_partner_far(piece, across, 1 - g, 1).start()

    def gather_copy(buf, send, recv, m, block, way):
        ref = buf.at[m, block]
        return remote(ref, ref, send.at[m, block, way], recv.at[m, block], (left, right)[way])

    def gather_step(buf, send, recv, m, step):
        @pl.when(s >= step)
        def _():
            block = s - step
            gather_copy(buf, send, recv, m, block, 1).wait_recv()

            @pl.when(has_right)
            def _():
                gather_copy(buf, send, recv, m, block, 1).start()

        @pl.when(s + step < seqs)
        def _():
            block = s + step
            gather_copy(buf, send, recv, m, block, 0).wait_recv()

            @pl.when(has_left)
            def _():
                gather_copy(buf, send, recv, m, block, 0).start()

    def gather_own(buf, send, recv, m):
        @pl.when(has_right)
        def _():
            gather_copy(buf, send, recv, m, s, 1).start()

        @pl.when(has_left)
        def _():
            gather_copy(buf, send, recv, m, s, 0).start()

    def gather_finish(buf, send, recv):
        for m in range(users):
            for block in range(seqs):
                @pl.when(jnp.logical_and(block <= s, has_right))
                def _():
                    gather_copy(buf, send, recv, m, block, 1).wait_send()

                @pl.when(jnp.logical_and(block >= s, has_left))
                def _():
                    gather_copy(buf, send, recv, m, block, 0).wait_send()

    loads["cand"].wait()
    loads["wq"].wait()
    for m in range(users):
        queries[m, s] = dot(cand[m], wq[...]).astype(BF16)
        if m == 0:
            pl.semaphore_wait(barrier, len(peers))
        gather_own(queries, q_send, q_recv, m)
    for piece in range(4):
        to_across(piece, u).start()
    for name in ("kv", "wg", "tm", "wo", "wu", "wd"):
        loads[name].start()
    for w in range(2):
        to_partner_own(w, u).start()

    loads["kv"].wait()
    for m in range(users):
        slots = s * hist + lax.broadcasted_iota(jnp.int32, (hist, 1), 0)
        visible = jnp.where(slots < len_ref[m], 1.0, 0.0)
        values[m] = (kv[m, :, inner:].astype(F32) * visible).astype(BF16)

    half_scale = 0.5 / math.sqrt(DH)

    def attend(m, block):
        for head in range(HEADS):
            cols = slice(head * DH, (head + 1) * DH)
            scores = lax.dot_general(
                queries[m, block, :, cols], kv[m, :, cols], (((1,), (1,)), ((), ())),
                preferred_element_type=F32,
            )
            weight = silu_of_double(scores * half_scale).astype(BF16)
            sums[m, block, :, cols] = dot(weight, values[m, :, cols])

    def partial_copy(m, block, way):
        return remote(
            outgoing.at[m, block], incoming.at[way, m, block],
            p_send.at[m, block], p_recv.at[way, m, block], (left, right)[way],
        )

    def pass_on(m, block, way, first):
        @pl.when(first)
        def _():
            outgoing[m, block] = sums[m, block].astype(BF16)

        @pl.when(jnp.logical_not(first))
        def _():
            partial_copy(m, block, way).wait_recv()
            outgoing[m, block] = (sums[m, block] + incoming[way, m, block].astype(F32)).astype(BF16)

        partial_copy(m, block, way).start()

    chip = lax.div(u, 2)
    quarter = rows // 4

    def quarter_rows(group, near):
        return pl.ds(pl.multiple_of((group * 2 + near) * quarter, quarter), quarter)

    def mix_copy(m):
        return remote(
            tm_hbm.at[quarter_rows(g, chip)], tm.at[s, quarter_rows(g, chip)],
            t_send.at[m], t_recv.at[s, 0], (g, first_owned + m, u),
        )

    def mix_share(block, which):
        part = tm.at[block, quarter_rows(g, 1 - chip if which == 3 else chip)]
        device = (g, s, across) if which == 1 else (1 - g, s, u)
        return remote(part, part, f_send.at[block, which], t_recv.at[block, which], device)

    def mix_arrived(block, which):
        part = tm.at[block, quarter_rows(1 - g if which > 1 else g, 1 - chip if which % 2 else chip)]
        remote(part, part, f_send.at[block, which], t_recv.at[block, which], (1 - g, s, u)).wait_recv()

    def for_far_blocks(do):
        for block in range(seqs):
            @pl.when(jnp.logical_and(is_owner, block != s))
            def _():
                do(block)

    def share_first(block):
        mix_arrived(block, 0)
        mix_share(block, 1).start()
        mix_share(block, 2).start()

    def share_second(block):
        mix_arrived(block, 1)
        mix_share(block, 3).start()

    def share_last(block):
        mix_arrived(block, 2)
        mix_arrived(block, 3)

    def share_sent(block):
        for which in (1, 2, 3):
            mix_share(block, which).wait_send()

    mirror = seqs - 1 - s
    def stage_of(step, m):
        if step < seqs:
            if step > 0:
                gather_step(queries, q_send, q_recv, m, step)

            @pl.when(s >= step)
            def _():
                attend(m, s - step)

            if step > 0:
                @pl.when(s + step < seqs)
                def _():
                    attend(m, s + step)

        owner = first_owned + m
        block = step - s

        @pl.when((owner > s) & (block >= 0) & (block < seqs))
        def _():
            pass_on(m, block, 1, s == 0)

        far = step - mirror

        @pl.when((owner < s) & (far >= 0) & (far < seqs))
        def _():
            pass_on(m, seqs - 1 - far, 0, mirror == 0)

    for step in range(2 * seqs - 2):
        for m in range(users):
            stage_of(step, m)

        if step == 0:
            loads["wg"].wait()
            for m in range(users):
                gates[m] = silu_of_double(dot(cand[m], wg[...]) * 0.5)
        if step == MIX_STEP:
            for m in range(users):
                @pl.when(first_owned + m != s)
                def _():
                    mix_copy(m).start()
        if step == SHARE_STEPS[0]:
            for_far_blocks(share_first)
        if step == SHARE_STEPS[1]:
            for_far_blocks(share_second)
        for piece in range(4):
            if step == ACROSS_STEPS[piece]:
                across_arrived(piece)
            if step == GROUP_STEPS[piece]:
                group_arrived(piece)

    def mixed_copy(block, m):
        return remote(
            mixed_out.at[block], mixed_in.at[m], m_send.at[block], m_recv.at[m], (g, block, u)
        )

    order = sorted(range(seqs), key=lambda block: min(block, seqs - 1 - block))
    loads["tm"].wait()
    for_far_blocks(share_last)

    @pl.when(is_owner)
    def _():
        for block in range(seqs):
            @pl.when(has_left)
            def _():
                partial_copy(owned, block, 1).wait_recv()
                sums[owned, block] = sums[owned, block] + incoming[1, owned, block].astype(F32)

            @pl.when(has_right)
            def _():
                partial_copy(owned, block, 0).wait_recv()
                sums[owned, block] = sums[owned, block] + incoming[0, owned, block].astype(F32)

            normed[block * rows:(block + 1) * rows] = layer_norm(sums[owned, block]).astype(BF16)
        for block in order:
            mixed = normed[block * rows:(block + 1) * rows].astype(F32) + dot(tm[block], normed[...])
            mixed_out[block] = mixed.astype(BF16)

            @pl.when(block != s)
            def _():
                mixed_copy(block, owned).start()

            @pl.when(block == s)
            def _():
                mixed_in[owned] = mixed.astype(BF16)

    for piece in range(4):
        if GROUP_STEPS[piece] >= 2 * seqs - 2:
            group_arrived(piece)
    loads["wo"].wait()
    ffn_ins = []
    for m in range(users):
        @pl.when(first_owned + m != s)
        def _():
            mixed_copy(s, m).wait_recv()

        gated = (mixed_in[m].astype(F32) * gates[m]).astype(BF16)
        state = cand[m].astype(F32) + dot(gated, wo[...])
        states[m * rows:(m + 1) * rows] = state
        ffn_ins.append(layer_norm(state).astype(BF16))
    ffn_in = jnp.concatenate(ffn_ins, axis=0)

    for w in range(2):
        loads[("wu", "wd")[w]].wait()
        to_partner_own(w, partner).wait_recv()
    for piece in range(4):
        to_partner_far(piece, across_partner, g, 0).wait_recv()
        to_partner_far(piece, across_partner, 1 - g, 1).wait_recv()
    total = states[...]
    for slot in range(hidden_slots):
        hidden = gelu_tanh(dot(ffn_in, wu[slot])).astype(BF16)
        total = total + dot(hidden, wd[slot])
    for m in range(users):
        out_ref[m] = total[m * rows:(m + 1) * rows].astype(BF16)

    gather_finish(queries, q_send, q_recv)
    for_far_blocks(share_sent)
    for m in range(users):
        @pl.when(first_owned + m != s)
        def _():
            mix_copy(m).wait_send()
            for block in range(seqs):
                partial_copy(m, block, 1).wait_send()

    @pl.when(is_owner)
    def _():
        for block in range(seqs):
            @pl.when(block != s)
            def _():
                mixed_copy(block, owned).wait_send()

    for w in range(2):
        to_partner_own(w, u).wait_send()
    for piece in range(4):
        to_across(piece, u).wait_send()
        to_group(piece, g).wait_send()
        to_partner_far(piece, across, g, 0).wait_send()
        to_partner_far(piece, across, 1 - g, 1).wait_send()


def fused(seqs, usrs, history_kv, candidates, lengths, w_query, w_gate, token_mix, w_out, w_up, w_down):
    users, hist, _ = history_kv.shape
    rows, width = candidates.shape[1:]
    inner = w_query.shape[1]
    depth = w_up.shape[1]
    dma = pltpu.SemaphoreType.DMA
    hbm = pl.BlockSpec(memory_space=pl.ANY)
    smem = pl.BlockSpec(memory_space=pltpu.SMEM)
    return pl.pallas_call(
        functools.partial(kernel, seqs),
        out_shape=jax.ShapeDtypeStruct(candidates.shape, BF16),
        in_specs=[hbm, hbm, smem, hbm, hbm, hbm, hbm, hbm, hbm],
        out_specs=pl.BlockSpec(memory_space=pltpu.VMEM),
        scratch_shapes=[
            pltpu.VMEM(history_kv.shape, BF16),
            pltpu.VMEM(candidates.shape, BF16),
            pltpu.VMEM(w_query.shape, BF16),
            pltpu.VMEM(w_gate.shape, BF16),
            pltpu.VMEM((seqs, *token_mix.shape), BF16),
            pltpu.VMEM(w_out.shape, BF16),
            pltpu.VMEM((usrs, width, depth), BF16),
            pltpu.VMEM((usrs, depth, width), BF16),
            pltpu.VMEM((users, hist, inner), BF16),
            pltpu.VMEM((users, seqs, rows, inner), BF16),
            pltpu.VMEM((users, seqs, rows, inner), F32),
            pltpu.VMEM((users, seqs, rows, inner), BF16),
            pltpu.VMEM((2, users, seqs, rows, inner), BF16),
            pltpu.VMEM((seqs * rows, inner), BF16),
            pltpu.VMEM((seqs, rows, inner), BF16),
            pltpu.VMEM((users, rows, inner), BF16),
            pltpu.VMEM((users, rows, inner), F32),
            pltpu.VMEM((users * rows, width), F32),
            dma((8,)),
            dma((users, seqs, 2)), dma((users, seqs)),
            dma((users, seqs)), dma((2, users, seqs)),
            dma((users,)), dma((seqs, 4)), dma((seqs, 4)), dma((seqs,)), dma((users,)),
            dma((2,)), dma((2,)), dma((4, 2)), dma((4, 2)),
            dma((4,)), dma((4,)), dma((4,)), dma((4,)),
        ],
        compiler_params=pltpu.CompilerParams(
            collective_id=0, has_side_effects=True, vmem_limit_bytes=56 * 1024 * 1024
        ),
        name="rank_layer",
    )(history_kv, candidates, lengths, w_query, w_gate, token_mix, w_out, w_up, w_down)


def shards(history_kv, candidates, lengths, w_query, w_gate, token_mix, w_out, w_up, w_down):
    user_count, hist_dev, _ = history_kv.shape
    inner = w_query.shape[1]
    half = hist_dev // 2
    scale = 1.0 / math.sqrt(DH)
    seq_index = lax.axis_index("seq")
    first_start = seq_index * hist_dev
    sections = ((history_kv[:, :half], first_start), (history_kv[:, half:], first_start + half))
    offsets = lax.iota(jnp.int32, half)
    queries = jnp.einsum(
        "ucd,de->uce", candidates, w_query, preferred_element_type=jnp.float32
    ).astype(jnp.bfloat16)
    piece = lax.all_gather(queries, "seq", axis=1, tiled=True)
    row_count = piece.shape[1]
    results = []
    for member in range(user_count):
        query_heads = piece[member].reshape(row_count, HEADS, DH)
        limit = lengths[member]
        summed = jnp.zeros((row_count, inner), jnp.float32)
        for section, section_start in sections:
            key_heads = section[member, :, :inner].reshape(half, HEADS, DH)
            value_heads = section[member, :, inner:].reshape(half, HEADS, DH)

            def compute(
                operand,
                key_heads=key_heads,
                value_heads=value_heads,
                section_start=section_start,
                query_heads=query_heads,
                limit=limit,
            ):
                scores = (
                    jnp.einsum(
                        "chd,thd->hct", query_heads, key_heads, preferred_element_type=jnp.float32
                    )
                    * scale
                )
                visible = section_start + offsets < limit
                weights = jnp.where(visible[None, None, :], jax.nn.silu(scores), 0.0).astype(
                    jnp.bfloat16
                )
                contrib = jnp.einsum(
                    "hct,thd->chd", weights, value_heads, preferred_element_type=jnp.float32
                )
                return contrib.reshape(row_count, inner)

            def skipped(operand):
                return jnp.zeros((row_count, inner), jnp.float32)

            summed = summed + lax.cond(section_start < limit, compute, skipped, 0)
        results.append(summed)
    partial_sums = jnp.stack(results)
    attended = lax.psum_scatter(partial_sums, "seq", scatter_dimension=1, tiled=True)
    normed = layer_norm(attended).astype(jnp.bfloat16)
    mixed = normed.astype(jnp.float32) + jnp.einsum(
        "cp,upe->uce",
        token_mix,
        lax.all_gather(normed, "seq", axis=1, tiled=True),
        preferred_element_type=jnp.float32,
    )
    gate_values = jax.nn.silu(
        jnp.einsum("ucd,de->uce", candidates, w_gate, preferred_element_type=jnp.float32)
    )
    gated = (mixed * gate_values).astype(jnp.bfloat16)
    state = candidates.astype(jnp.float32) + jnp.einsum(
        "uce,ed->ucd", gated, w_out, preferred_element_type=jnp.float32
    )
    ffn_in = layer_norm(state).astype(jnp.bfloat16)
    hidden = jax.nn.gelu(
        jnp.einsum(
            "ucd,df->ucf",
            lax.all_gather(ffn_in, "usr", axis=0, tiled=True),
            w_up,
            preferred_element_type=jnp.float32,
        )
    ).astype(jnp.bfloat16)
    ffn_terms = jnp.einsum("ucf,fd->ucd", hidden, w_down, preferred_element_type=jnp.float32)
    ffn_out = lax.psum_scatter(
        ffn_terms.astype(jnp.bfloat16), "usr", scatter_dimension=0, tiled=True
    ).astype(jnp.float32)
    return (state + ffn_out).astype(jnp.bfloat16)


def solution(mesh):
    sizes = dict(mesh.shape)
    seqs, usrs = sizes["seq"], sizes["usr"]
    def body(history_kv, candidates, *rest):
        operands = (history_kv, candidates, *rest)
        if sizes["grp"] == 2 and usrs == 4 and seqs == 2 * candidates.shape[0] and seqs >= 4:
            return fused(seqs, usrs, *operands)
        return shards(*operands)

    return jax.shard_map(
        body,
        mesh=mesh,
        in_specs=(
            P(("grp", "usr"), "seq", None),
            P(("grp", "usr"), "seq", None),
            P(("grp", "usr")),
            P(),
            P(),
            P("seq", None),
            P(),
            P(None, "usr"),
            P("usr", None),
        ),
        out_specs=P(("grp", "usr"), "seq", None),
        check_vma=False,
    )
```
